32 devices in a mesh: prow: 4 (over y, core), pcol: 8 (over z, x).
Axes of the slice: x: 2, y: 2, z: 4, core: 2. Of those that a mesh axis runs over, the one named last changes fastest.
Arguments:
- covariance: bfloat16 [2, 4, 4, 512, 2, 8, 512], P(None, None, 'prow', None, None, 'pcol'), may hold values from 0 to 2, as said below
Outputs:
- factored: float32 [2, 4, 4, 512, 2, 8, 512], P(None, None, 'prow', None, None, 'pcol')
The draws below stay inside these ranges and needn't reach their ends.
Inputs may be any that keep to these rules, and one draw needn't show every extreme that they name: For each candidate a symmetric positive definite Matern covariance of scattered observations (smoothness 1/2, 3/2 or 5/2) plus a positive nugget on the diagonal.
All inputs are finite; a program needn't handle non-finite values.
Results may differ from the reference program's by a relative error of at most 0.0019.
Values may be sent and summed in bfloat16 or wider, within the bound.
A program may use at most 192 MiB of HBM per device.

```python
import math
import jax
import jax.numpy as jnp
from jax import lax

NB = 512
FACTORED = 2
CAND = 2
LC = 2
LR = 4
M = 8192


def draw_covariance(key, part):
    subkeys = jax.random.split(jax.random.fold_in(key, 11), 5)
    side_length = math.sqrt(M)
    coords = jax.random.uniform(subkeys[0], (CAND, 2, M), jnp.float32) * side_length
    length = side_length * jnp.exp(jax.random.uniform(subkeys[1], (CAND,), jnp.float32, math.log(0.08), math.log(0.25)))
    variance = jnp.exp(jax.random.uniform(subkeys[2], (CAND,), jnp.float32, math.log(0.7), math.log(1.4)))
    nugget = jax.random.uniform(subkeys[3], (CAND,), jnp.float32, 0.3, 0.5)
    smooth = jax.random.randint(subkeys[4], (CAND,), 0, 3)

    def one_block(block_index):
        first_row = block_index * NB
        near_points = lax.dynamic_slice_in_dim(coords, first_row, NB, 2)
        delta_x = near_points[:, 0, :, None] - coords[:, 0, None, :]
        delta_y = near_points[:, 1, :, None] - coords[:, 1, None, :]
        scaled = jnp.sqrt(delta_x * delta_x + delta_y * delta_y) / length[:, None, None]
        kernel_half = jnp.exp(-scaled)
        kernel_three = (1.0 + math.sqrt(3.0) * scaled) * jnp.exp(-math.sqrt(3.0) * scaled)
        kernel_five = (1.0 + math.sqrt(5.0) * scaled + 5.0 * scaled * scaled / 3.0) * jnp.exp(-math.sqrt(5.0) * scaled)
        code = smooth[:, None, None]
        kernel = jnp.where(code == 0, kernel_half, jnp.where(code == 1, kernel_three, kernel_five))
        same_point = (first_row + jnp.arange(NB))[:, None] == jnp.arange(M)[None, :]
        entries = variance[:, None, None] * kernel + jnp.where(same_point[None], nugget[:, None, None], 0.0)
        return entries.astype(jnp.bfloat16)
    stacked = lax.map(one_block, jnp.arange(M // NB))
    whole = jnp.transpose(stacked, (1, 0, 2, 3)).reshape(CAND, M, M)
    return whole.reshape(CAND, LR, M // (LR * NB), NB, LC, M // (LC * NB), NB)


def setup_inputs(seed: int = 0) -> dict:
    arg_keys = jax.random.split(jax.random.key(seed), 2)
    return {
        "covariance": draw_covariance(jax.random.fold_in(arg_keys[1], 71), 0),
    }


def factor_one(matrix):
    matrix = matrix.astype(jnp.float32)
    row_index = jnp.arange(M)
    columns = []
    for tile_step in range(FACTORED):
        start_row = tile_step * NB
        diag_block = matrix[start_row:start_row + NB, start_row:start_row + NB]
        lower_factor = jnp.linalg.cholesky(diag_block)
        solved = lax.linalg.triangular_solve(lower_factor, matrix[:, start_row:start_row + NB], left_side=False, lower=True, transpose_a=True)
        below_mask = (row_index >= start_row + NB)[:, None]
        panel_rows = jnp.where(below_mask, solved, 0.0)
        columns.append(panel_rows.at[start_row:start_row + NB].set(lower_factor))
        rounded = panel_rows.astype(jnp.bfloat16)
        matrix = matrix - jnp.dot(rounded.astype(jnp.float32), rounded.T.astype(jnp.float32), preferred_element_type=jnp.float32)
    factored_cols = FACTORED * NB
    upper_mask = (row_index < factored_cols)[:, None]
    right_part = jnp.where(upper_mask, 0.0, matrix[:, factored_cols:])
    return jnp.concatenate(columns + [right_part], axis=1)

def reference(covariance):
    whole = covariance.reshape(CAND, M, M)
    result = jnp.stack([factor_one(whole[candidate]) for candidate in range(CAND)])
    return result.reshape(covariance.shape)
```

```python
import functools

import jax
import jax.numpy as jnp
from jax import lax
from jax.experimental import pallas as pl
from jax.experimental.pallas import tpu as pltpu
from jax.sharding import PartitionSpec as P

FACTORED = 2
BLOCK = 128
STRIP = 8
HIGH = lax.Precision.HIGHEST


def dot_t(a, b):
    return lax.dot_general(a, b, (((0,), (0,)), ((), ())), precision=HIGH, preferred_element_type=jnp.float32)


def factor_kernel(a_ref, upper_ref, inverse_ref, work, diag):
    cands, side, _ = a_ref.shape
    blocks = side // BLOCK
    eye_row = lax.broadcasted_iota(jnp.int32, (BLOCK, BLOCK), 0)
    eye_col = lax.broadcasted_iota(jnp.int32, (BLOCK, BLOCK), 1)
    eye = (eye_row == eye_col).astype(jnp.float32)
    sub_narrow = lax.broadcasted_iota(jnp.int32, (STRIP, BLOCK), 0)
    sub_wide = lax.broadcasted_iota(jnp.int32, (STRIP, 2 * BLOCK), 0)
    lane = lax.broadcasted_iota(jnp.int32, (STRIP, BLOCK), 1)
    for c in range(cands):
        work[c, :, :side] = a_ref[c]
        work[c, :, side:] = jnp.zeros((side, side), jnp.float32)
        for block in range(blocks):
            rows = slice(block * BLOCK, (block + 1) * BLOCK)
            work[c, rows, side + block * BLOCK : side + (block + 1) * BLOCK] = eye
    for block in range(blocks):
        lo = block * BLOCK
        hi = lo + BLOCK
        for c in range(cands):
            diag[c, :, :BLOCK] = work[c, lo:hi, lo:hi]
            diag[c, :, BLOCK:] = eye

        def strip_step(step, carry):
            start = pl.multiple_of(step * STRIP, STRIP)
            strips = [diag[c, pl.ds(start, STRIP), :] for c in range(cands)]
            turned = [
                pltpu.roll(strip[:, :BLOCK], lax.rem(BLOCK - start, BLOCK), 1) for strip in strips
            ]
            for t in range(STRIP):
                for c in range(cands):
                    column = jnp.broadcast_to(turned[c][:, t : t + 1], (STRIP, BLOCK))
                    scale = lax.rsqrt(jnp.broadcast_to(column[t : t + 1], (STRIP, BLOCK)))
                    factor = column * (scale * scale)
                    wide_factor = jnp.concatenate([factor, factor], axis=1)
                    wide_scale = jnp.concatenate([scale, scale], axis=1)
                    row = turned[c][t : t + 1]
                    wide_row = strips[c][t : t + 1]
                    turned[c] = jnp.where(
                        sub_narrow > t, turned[c] - factor * row, turned[c]
                    )
                    strips[c] = jnp.where(
                        sub_wide > t,
                        strips[c] - wide_factor * wide_row,
                        jnp.where(sub_wide == t, strips[c] * wide_scale, strips[c]),
                    )
            for c in range(cands):
                diag[c, pl.ds(start, STRIP), :] = strips[c]
            for c in range(cands):
                later = jnp.where(lane >= start + STRIP, strips[c][:, :BLOCK], 0.0)
                diag[c] = diag[c] - dot_t(later, strips[c])
            return carry

        lax.fori_loop(0, BLOCK // STRIP, strip_step, 0)
        for c in range(cands):
            small = jnp.where(eye_row >= eye_col, diag[c, :, BLOCK:], 0.0)
            done = jnp.dot(
                small, work[c, lo:hi, lo : side + hi],
                precision=HIGH, preferred_element_type=jnp.float32,
            )
            upper_ref[c, lo:hi, lo:side] = done[:, : side - lo]
            upper_ref[c, lo:hi, lo:hi] = jnp.where(
                eye_row <= eye_col, diag[c, :, :BLOCK], 0.0
            )
            if lo:
                upper_ref[c, lo:hi, :lo] = jnp.zeros((BLOCK, lo), jnp.float32)
            inverse_ref[c, lo:hi, :hi] = done[:, side - lo :]
            if hi < side:
                inverse_ref[c, lo:hi, hi:] = jnp.zeros((BLOCK, side - hi), jnp.float32)
                work[c, hi:, hi : side + hi] = work[c, hi:, hi : side + hi] - dot_t(
                    done[:, BLOCK : side - lo], done[:, BLOCK:]
                )


def factor(matrix):
    cands, side, _ = matrix.shape
    shape = jax.ShapeDtypeStruct(matrix.shape, jnp.float32)
    vmem = pl.BlockSpec(memory_space=pltpu.VMEM)
    return pl.pallas_call(
        factor_kernel,
        out_shape=(shape, shape),
        in_specs=[vmem],
        out_specs=(vmem, vmem),
        scratch_shapes=[
            pltpu.VMEM((cands, side, 2 * side), jnp.float32),
            pltpu.VMEM((cands, BLOCK, 2 * BLOCK), jnp.float32),
        ],
        cost_estimate=pl.CostEstimate(
            flops=40_000_000_000, bytes_accessed=8 * side * side * cands, transcendentals=0
        ),
        name="factor",
    )(matrix)


def halves(value):
    high = lax.reduce_precision(value, 8, 7)
    return high.astype(jnp.bfloat16), (value - high).astype(jnp.bfloat16)


def product(form, a, b, precision=None):
    return jnp.einsum(form, a, b, precision=precision, preferred_element_type=jnp.float32)


def shards(covariance):
    cands, row_tiles, _, side, column_tiles = covariance.shape[:5]
    prows = lax.axis_size("prow")
    pcols = lax.axis_size("pcol")
    ratio = pcols // prows
    grid_row = lax.axis_index("prow")
    grid_column = lax.axis_index("pcol")
    rows = row_tiles * side
    columns = column_tiles * side
    base = covariance.reshape(cands, rows, columns)
    row_global = jnp.arange(rows) // side * prows + grid_row
    column_global = jnp.arange(columns) // side * pcols + grid_column

    tile = base[:, :side, :side]
    at = lambda p, q: (grid_row == p) & (grid_column == q)
    zero = jnp.zeros_like(tile)
    first = lax.psum(jnp.where(at(0, 0), tile, zero), ("prow", "pcol"))
    second = lax.psum(
        jnp.stack([jnp.where(at(0, 1), tile, zero), jnp.where(at(1, 1), tile, zero)]),
        ("pcol", "prow"),
    )

    pieces = prows // FACTORED
    flat = base[:, :side, :].reshape(pieces, cands * side // pieces, columns)
    piece = flat[0]
    for s in range(1, pieces):
        moved = lax.ppermute(
            flat[s], "prow", [(k, FACTORED * s + k) for k in range(FACTORED)]
        )
        piece = jnp.where(grid_row // FACTORED == s, moved, piece)
    spread = lax.all_gather(piece, "prow")
    column_raw = (
        spread.reshape(pieces, FACTORED, -1, columns)
        .transpose(1, 0, 2, 3)
        .reshape(FACTORED, cands, side, columns)
    )
    turned = lax.ppermute(
        piece,
        ("prow", "pcol"),
        [
            (p * pcols + q, (q % prows) * pcols + p * ratio + q // prows)
            for p in range(prows)
            for q in range(pcols)
        ],
    )
    gathered = lax.all_gather(turned, "pcol")
    row_raw = (
        gathered.reshape(pieces, FACTORED, ratio, -1, column_tiles, side)
        .transpose(1, 0, 3, 4, 2, 5)
        .reshape(FACTORED, cands, side, rows)
    )
    raw = jnp.concatenate([row_raw, column_raw], axis=3)
    every = jnp.concatenate([row_global, column_global])

    upper0, inverse0 = factor(first.astype(jnp.float32))
    near = product("cij,cjk->cik", inverse0, second[0].astype(jnp.float32), HIGH)
    near = lax.reduce_precision(near, 8, 7).astype(jnp.bfloat16)
    upper1, inverse1 = factor(
        second[1].astype(jnp.float32) - product("ckr,cks->crs", near, near)
    )
    mixed = product("cij,ckj->cik", inverse1, near.astype(jnp.float32), HIGH)

    high, low = halves(inverse0)
    solved0 = product("cij,cjk->cik", high, raw[0]) + product("cij,cjk->cik", low, raw[0])
    rounded0 = jnp.where(every > 0, solved0, 0.0).astype(jnp.bfloat16)
    high, low = halves(jnp.concatenate([inverse1, -mixed], axis=2))
    both = jnp.concatenate([raw[1], rounded0], axis=1)
    solved1 = product("cij,cjk->cik", high, both) + product("cij,cjk->cik", low, both)
    rounded1 = jnp.where(every > 1, solved1, 0.0).astype(jnp.bfloat16)
    rounded = jnp.concatenate([rounded0, rounded1], axis=1)
    result = base.astype(jnp.float32) - product(
        "ckr,cks->crs", rounded[:, :, :rows], rounded[:, :, rows:]
    )

    mine = jnp.where(grid_column == 0, solved0[:, :, :rows], solved1[:, :, :rows])
    upper = jnp.where(grid_column == 0, upper0, upper1)
    mine = jnp.where(row_global > grid_column, mine, 0.0)
    mine = mine.at[:, :, :side].set(
        jnp.where(grid_row == grid_column, upper, mine[:, :, :side])
    )
    mine = jnp.swapaxes(mine, 1, 2)
    head = jnp.where(grid_column < FACTORED, mine, result[:, :, :side])
    result = jnp.concatenate([head, result[:, :, side:]], axis=2)
    upper_mask = (row_global[:, None] < FACTORED) & (column_global[None, :] >= FACTORED)
    result = jnp.where(upper_mask[None], 0.0, result)
    return result.reshape(covariance.shape)


def solution(mesh):
    placed = P(None, None, "prow", None, None, "pcol", None)
    return jax.shard_map(
        shards, mesh=mesh, in_specs=(placed,), out_specs=placed, check_vma=False
    )
```

```python
import functools

import jax
import jax.numpy as jnp
from jax import lax
from jax.experimental import pallas as pl
from jax.experimental.pallas import tpu as pltpu
from jax.sharding import PartitionSpec as P

FACTORED = 2
BLOCK = 128
STRIP = 8
HIGH = lax.Precision.HIGHEST


def dot_t(a, b):
    return lax.dot_general(a, b, (((0,), (0,)), ((), ())), precision=HIGH, preferred_element_type=jnp.float32)


def factor_kernel(a_ref, upper_ref, inverse_ref, work, diag):
    cands, side, _ = a_ref.shape
    blocks = side // BLOCK
    eye_row = lax.broadcasted_iota(jnp.int32, (BLOCK, BLOCK), 0)
    eye_col = lax.broadcasted_iota(jnp.int32, (BLOCK, BLOCK), 1)
    eye = (eye_row == eye_col).astype(jnp.float32)
    sub_narrow = lax.broadcasted_iota(jnp.int32, (STRIP, BLOCK), 0)
    sub_wide = lax.broadcasted_iota(jnp.int32, (STRIP, 2 * BLOCK), 0)
    lane = lax.broadcasted_iota(jnp.int32, (STRIP, BLOCK), 1)
    for c in range(cands):
        work[c, :, :side] = a_ref[c]
        work[c, :, side:] = jnp.zeros((side, side), jnp.float32)
        for block in range(blocks):
            rows = slice(block * BLOCK, (block + 1) * BLOCK)
            work[c, rows, side + block * BLOCK : side + (block + 1) * BLOCK] = eye
    for block in range(blocks):
        lo = block * BLOCK
        hi = lo + BLOCK
        for c in range(cands):
            diag[c, :, :BLOCK] = work[c, lo:hi, lo:hi]
            diag[c, :, BLOCK:] = eye

        def strip_step(step, carry):
            start = pl.multiple_of(step * STRIP, STRIP)
            strips = [diag[c, pl.ds(start, STRIP), :] for c in range(cands)]
            turned = [
                pltpu.roll(strip[:, :BLOCK], lax.rem(BLOCK - start, BLOCK), 1) for strip in strips
            ]
            for t in range(STRIP):
                for c in range(cands):
                    column = jnp.broadcast_to(turned[c][:, t : t + 1], (STRIP, BLOCK))
                    scale = lax.rsqrt(jnp.broadcast_to(column[t : t + 1], (STRIP, BLOCK)))
                    factor = column * (scale * scale)
                    wide_factor = jnp.concatenate([factor, factor], axis=1)
                    wide_scale = jnp.concatenate([scale, scale], axis=1)
                    row = turned[c][t : t + 1]
                    wide_row = strips[c][t : t + 1]
                    turned[c] = jnp.where(
                        sub_narrow > t, turned[c] - factor * row, turned[c]
                    )
                    strips[c] = jnp.where(
                        sub_wide > t,
                        strips[c] - wide_factor * wide_row,
                        jnp.where(sub_wide == t, strips[c] * wide_scale, strips[c]),
                    )
            for c in range(cands):
                diag[c, pl.ds(start, STRIP), :] = strips[c]
            for c in range(cands):
                later = jnp.where(lane >= start + STRIP, strips[c][:, :BLOCK], 0.0)
                diag[c] = diag[c] - dot_t(later, strips[c])
            return carry

        lax.fori_loop(0, BLOCK // STRIP, strip_step, 0)
        for c in range(cands):
            small = jnp.where(eye_row >= eye_col, diag[c, :, BLOCK:], 0.0)
            done = jnp.dot(
                small, work[c, lo:hi, lo : side + hi],
                precision=HIGH, preferred_element_type=jnp.float32,
            )
            upper_ref[c, lo:hi, lo:side] = done[:, : side - lo]
            upper_ref[c, lo:hi, lo:hi] = jnp.where(
                eye_row <= eye_col, diag[c, :, :BLOCK], 0.0
            )
            if lo:
                upper_ref[c, lo:hi, :lo] = jnp.zeros((BLOCK, lo), jnp.float32)
            inverse_ref[c, lo:hi, :hi] = done[:, side - lo :]
            if hi < side:
                inverse_ref[c, lo:hi, hi:] = jnp.zeros((BLOCK, side - hi), jnp.float32)
                work[c, hi:, hi : side + hi] = work[c, hi:, hi : side + hi] - dot_t(
                    done[:, BLOCK : side - lo], done[:, BLOCK:]
                )


def factor(matrix):
    cands, side, _ = matrix.shape
    shape = jax.ShapeDtypeStruct(matrix.shape, jnp.float32)
    vmem = pl.BlockSpec(memory_space=pltpu.VMEM)
    return pl.pallas_call(
        factor_kernel,
        out_shape=(shape, shape),
        in_specs=[vmem],
        out_specs=(vmem, vmem),
        scratch_shapes=[
            pltpu.VMEM((cands, side, 2 * side), jnp.float32),
            pltpu.VMEM((cands, BLOCK, 2 * BLOCK), jnp.float32),
        ],
        cost_estimate=pl.CostEstimate(
            flops=40_000_000_000, bytes_accessed=8 * side * side * cands, transcendentals=0
        ),
        name="factor",
    )(matrix)


def halves(value):
    high = lax.reduce_precision(value, 8, 7)
    return high.astype(jnp.bfloat16), (value - high).astype(jnp.bfloat16)


def product(form, a, b, precision=None):
    return jnp.einsum(form, a, b, precision=precision, preferred_element_type=jnp.float32)


def shards(covariance):
    cands, row_tiles, _, side, column_tiles = covariance.shape[:5]
    prows = lax.axis_size("prow")
    pcols = lax.axis_size("pcol")
    ratio = pcols // prows
    grid_row = lax.axis_index("prow")
    grid_column = lax.axis_index("pcol")
    rows = row_tiles * side
    columns = column_tiles * side
    base = covariance.reshape(cands, rows, columns)
    row_global = jnp.arange(rows) // side * prows + grid_row
    column_global = jnp.arange(columns) // side * pcols + grid_column

    tile = base[:, :side, :side]
    at = lambda p, q: (grid_row == p) & (grid_column == q)
    zero = jnp.zeros_like(tile)
    first = lax.psum(jnp.where(at(0, 0), tile, zero), ("prow", "pcol"))
    first, tile = lax.optimization_barrier((first, tile))
    second = lax.psum(
        jnp.stack([jnp.where(at(0, 1), tile, zero), jnp.where(at(1, 1), tile, zero)]),
        ("prow", "pcol"),
    )

    pieces = prows // FACTORED
    flat = base[:, :side, :].reshape(pieces, cands * side // pieces, columns)
    piece = flat[0]
    for s in range(1, pieces):
        moved = lax.ppermute(
            flat[s], "prow", [(k, FACTORED * s + k) for k in range(FACTORED)]
        )
        piece = jnp.where(grid_row // FACTORED == s, moved, piece)
    turned = lax.ppermute(
        piece,
        ("prow", "pcol"),
        [
            (p * pcols + q, (q % prows) * pcols + p * ratio + q // prows)
            for p in range(prows)
            for q in range(pcols)
        ],
    )
    spread = jnp.zeros((prows,) + piece.shape, piece.dtype)
    spread = lax.dynamic_update_index_in_dim(spread, piece, grid_row, 0)
    for d in range(1, prows):
        moved = lax.ppermute(piece, "prow", [(p, (p + d) % prows) for p in range(prows)])
        spread = lax.dynamic_update_index_in_dim(
            spread, moved, (grid_row - d + prows) % prows, 0
        )
    spread = spread.reshape(pieces, FACTORED, -1, columns)
    second, turned = lax.optimization_barrier((second, turned))
    gathered = lax.all_gather(turned, "pcol")
    gathered = gathered.reshape(pieces, FACTORED, ratio, -1, columns)
    groups = [
        ([gathered[:, k, b].reshape(cands, side, columns) for k in range(FACTORED)],
         (jnp.arange(columns) // side * ratio + b) * prows + grid_row)
        for b in range(ratio)
    ]
    groups.append(
        ([spread[:, k].reshape(cands, side, columns) for k in range(FACTORED)], column_global)
    )

    upper0, inverse0 = factor(first.astype(jnp.float32))
    near = product("cij,cjk->cik", inverse0, second[0].astype(jnp.float32), HIGH)
    near = lax.reduce_precision(near, 8, 7).astype(jnp.bfloat16)
    upper1, inverse1 = factor(
        second[1].astype(jnp.float32) - product("ckr,cks->crs", near, near)
    )
    mixed = product("cij,ckj->cik", inverse1, near.astype(jnp.float32), HIGH)

    high0, low0 = halves(inverse0)
    high1, low1 = halves(jnp.concatenate([inverse1, -mixed], axis=2))
    solved = []
    rounded = []
    for raw, place in groups:
        solved0 = product("cij,cjk->cik", high0, raw[0]) + product("cij,cjk->cik", low0, raw[0])
        rounded0 = jnp.where(place > 0, solved0, 0.0).astype(jnp.bfloat16)
        both = jnp.concatenate([raw[1], rounded0], axis=1)
        solved1 = product("cij,cjk->cik", high1, both) + product("cij,cjk->cik", low1, both)
        rounded1 = jnp.where(place > 1, solved1, 0.0).astype(jnp.bfloat16)
        solved.append(jnp.where(grid_column == 0, solved0, solved1))
        rounded.append(jnp.concatenate([rounded0, rounded1], axis=1))

    def in_order(parts):
        parts = [part.reshape(part.shape[:2] + (column_tiles, 1, side)) for part in parts]
        return jnp.concatenate(parts, axis=3).reshape(parts[0].shape[:2] + (rows,))

    result = base.astype(jnp.float32) - product(
        "ckr,cks->crs", in_order(rounded[:ratio]), rounded[ratio]
    )

    mine = jnp.where(row_global > grid_column, in_order(solved[:ratio]), 0.0)
    upper = jnp.where(grid_column == 0, upper0, upper1)
    mine = mine.at[:, :, :side].set(
        jnp.where(grid_row == grid_column, upper, mine[:, :, :side])
    )
    mine = jnp.swapaxes(mine, 1, 2)[:, :, None, :]
    result = result.reshape(cands, rows, column_tiles, side)
    tile_global = (jnp.arange(column_tiles) * pcols + grid_column)[None, None, :, None]
    row_global = row_global[None, :, None, None]
    result = jnp.where((row_global < FACTORED) & (tile_global >= FACTORED), 0.0, result)
    result = jnp.where(tile_global < FACTORED, mine, result)
    return result.reshape(covariance.shape)


def solution(mesh):
    placed = P(None, None, "prow", None, None, "pcol", None)
    return jax.shard_map(
        shards, mesh=mesh, in_specs=(placed,), out_specs=placed, check_vma=False
    )
```
